32 devices in a mesh: lead: 8 (over z, x), space: 4 (over y, core).
Axes of the slice: x: 2, y: 2, z: 4, core: 2. Of those that a mesh axis runs over, the one named last changes fastest.
Arguments:
- latents: bfloat16 [8, 64, 128, 1024], P('lead', 'space'), may hold values from -6 to 6
- owners: int32 [2], replicated, may hold values from 0 to 7, as said below
- lead_ids: int32 [8], P('lead'), may hold values from 0 to 359
- film_scale: float32 [360, 1024], replicated, may hold values from -3 to 3
- film_shift: float32 [360, 1024], replicated, may hold values from -3 to 3
- w_qkv_row: bfloat16 [1024, 3072], P('space'), may hold values from -0.1875 to 0.1875
- w_out_row: bfloat16 [1024, 1024], P('space'), may hold values from -0.1875 to 0.1875
- gain_col: float32 [1024], replicated, may hold values from 0.25 to 1.75
- w_qkv_col: bfloat16 [1024, 3072], P('space'), may hold values from -0.1875 to 0.1875
- w_out_col: bfloat16 [1024, 1024], P('space'), may hold values from -0.1875 to 0.1875
Outputs:
- result: bfloat16 [8, 64, 128, 1024], P('lead', None, 'space')
The draws below stay inside these ranges and needn't reach their ends.
Inputs may be any that keep to these rules, and one draw needn't show every extreme that they name: `owners`: the two analysis times are held by two different lead groups, one of which is the last lead group.
All inputs are finite; a program needn't handle non-finite values.
Results may differ from the reference program's by a relative error of at most 0.013.
Values may be sent and summed in bfloat16 or wider, within the bound.
No kernel may reach another device: no remote copies, remote signals or barrier semaphores. Data moves between devices by JAX's collectives and lax.ppermute only.
A program may use at most 128 MiB of HBM per device.

```python
import jax
import jax.numpy as jnp
from jax import lax

C = 1024
HEADS = 8
H = 64
W = 128
NLEADS = 360
N_LEAD = 8


def draw_owners(key, part):
    other = jax.random.randint(jax.random.fold_in(key, 11), (), 0, N_LEAD - 1).astype(jnp.int32)
    last = jnp.int32(N_LEAD - 1)
    flip = jax.random.randint(jax.random.fold_in(key, 12), (), 0, 2).astype(jnp.int32)
    first = jnp.where(flip == 1, last, other)
    second = jnp.where(flip == 1, other, last)
    return jnp.stack([first, second]).astype(jnp.int32)


def with_ends(result, key, low, high):
    dims = result.shape
    place = [jax.random.randint(jax.random.fold_in(key, axis), (), 0, dims[axis]) for axis in range(len(dims))]
    result = result.at[tuple(place)].set(low)
    longest = dims.index(max(dims))
    place[longest] = (place[longest] + 1) % dims[longest]
    return result.at[tuple(place)].set(high)


def level_of(key, extent, cuts, least, largest):
    factor_of = 1.0
    for dim, shards_of in cuts:
        steps = jax.random.uniform(jax.random.fold_in(jax.random.fold_in(key, 6), dim), (shards_of,), jnp.float32, least / len(cuts), largest / len(cuts))
        factor_of = factor_of * jnp.repeat(jnp.exp(steps), extent[dim] // shards_of).reshape((-1,) + (1,) * (len(extent) - 1 - dim))
    return factor_of


def centred(stream_key, shape, scale, bound, shards=(), kind=jnp.bfloat16):
    array = jax.random.normal(stream_key, shape, jnp.float32) * scale
    if len(shards) > 0:
        array = level_of(stream_key, shape, shards, -0.22, 0.18) * array
    return jnp.clip(array, min=-bound, max=bound).astype(kind)


def setup_inputs(seed: int = 0) -> dict:
    seeds = jax.random.split(jax.random.key(seed), 11)
    return {
        "latents": centred(seeds[0], (N_LEAD, H, W, C), 1.0, 6.0, ((0, 8), (1, 4))),
        "owners": draw_owners(jax.random.fold_in(seeds[10], 71), 0),
        "lead_ids": with_ends(jax.random.randint(seeds[2], (N_LEAD,), 0, NLEADS), jax.random.fold_in(seeds[2], 1), 0, NLEADS - 1).astype(jnp.int32),
        "film_scale": centred(seeds[3], (NLEADS, C), 0.5, 3.0, (), jnp.float32),
        "film_shift": centred(seeds[4], (NLEADS, C), 0.5, 3.0, (), jnp.float32),
        "w_qkv_row": centred(seeds[5], (C, 3 * C), C ** -0.5, 0.1875, ((0, 4),)),
        "w_out_row": centred(seeds[6], (C, C), C ** -0.5, 0.1875, ((0, 4),)),
        "gain_col": jnp.clip(1.0 + 0.15 * jax.random.normal(seeds[7], (C,), jnp.float32), 0.25, 1.75),
        "w_qkv_col": centred(seeds[8], (C, 3 * C), C ** -0.5, 0.1875, ((0, 4),)),
        "w_out_col": centred(seeds[9], (C, C), C ** -0.5, 0.1875, ((0, 4),)),
    }


def rms_norm(values):
    return values * lax.rsqrt(lax.optimization_barrier(jnp.mean(values * values, axis=-1, keepdims=True)) + 1e-06)

def attend(tokens, w_qkv, w_out):
    batch, length, channels = tokens.shape
    head_dim = channels // HEADS
    projected = jnp.dot(tokens.reshape(-1, channels), w_qkv, preferred_element_type=jnp.float32).astype(jnp.bfloat16)
    projected = projected.reshape(batch, length, 3, HEADS, head_dim).astype(jnp.float32)
    queries = projected[:, :, 0]
    key_heads = projected[:, :, 1]
    values = projected[:, :, 2]
    scores = jnp.einsum('bihd,bjhd->bhij', queries, key_heads) / jnp.sqrt(jnp.float32(head_dim))
    weights_soft = jax.nn.softmax(scores, axis=-1).astype(jnp.bfloat16).astype(jnp.float32)
    mixed = jnp.einsum('bhij,bjhd->bihd', weights_soft, values).astype(jnp.bfloat16)
    outcome = jnp.dot(mixed.reshape(-1, channels), w_out, preferred_element_type=jnp.float32)
    return outcome.reshape(batch, length, channels)

def reference(latents, owners, lead_ids, film_scale, film_shift, w_qkv_row, w_out_row, gain_col, w_qkv_col, w_out_col):
    summed = latents[owners[0]].astype(jnp.float32) + latents[owners[1]].astype(jnp.float32)
    normal_base = rms_norm(summed)

    def one_lead(lead_time):
        hidden = (normal_base * (1.0 + film_scale[lead_time]) + film_shift[lead_time]).astype(jnp.bfloat16)
        after_rows = (hidden.astype(jnp.float32) + attend(hidden, w_qkv_row, w_out_row)).astype(jnp.bfloat16)
        normed = (rms_norm(after_rows.astype(jnp.float32)) * gain_col).astype(jnp.bfloat16)
        column_out = attend(jnp.transpose(normed, (1, 0, 2)), w_qkv_col, w_out_col)
        return (after_rows.astype(jnp.float32) + jnp.transpose(column_out, (1, 0, 2))).astype(jnp.bfloat16)
    return lax.map(one_lead, lead_ids)
```

```python
import math

import jax
import jax.numpy as jnp
from jax import lax
from jax.experimental import pallas as pl
from jax.experimental.pallas import tpu as pltpu
from jax.sharding import PartitionSpec as P

HEADS = 8
EPS = 1e-06
NEG = -1e30
BLOCK = 128
TILE = 512
F32 = jnp.float32
BF16 = jnp.bfloat16


def dot(a, b):
    return jnp.dot(a, b, preferred_element_type=F32)


def dot_t(a, b):
    return lax.dot_general(a, b, (((1,), (1,)), ((), ())), preferred_element_type=F32)


def attention(n_tiles, tokens, load, w_qkv_ref, w_out_ref, mix_ref, finish, keep):
    channels = w_out_ref.shape[0]
    head = channels // HEADS
    pair = 2 * head
    factor = math.log2(math.e) / math.sqrt(head)
    units = [
        (slice(b * BLOCK, (b + 1) * BLOCK), slice(j * head, (j + 1) * head))
        for b in range(tokens // BLOCK)
        for j in range(2)
    ]
    steps = [(t, p) for t in range(n_tiles) for p in range(HEADS // 2)]

    def project(step):
        t, p = step
        x = load(t)
        return [
            dot(x, w_qkv_ref[:, c * channels + p * pair : c * channels + (p + 1) * pair]).astype(BF16)
            for c in range(3)
        ]

    def soften(scores):
        if keep is not None:
            scores = jnp.where(keep, scores, NEG)
        top = jnp.max(scores, axis=-1, keepdims=True)
        return jnp.exp2((scores - top) * factor).astype(BF16)

    ahead = project(steps[0])
    for n, (t, p) in enumerate(steps):
        q, k, v = ahead
        scores = [dot_t(q[r, c], k[r, c]) for r, c in units]
        if n + 1 < len(steps):
            ahead = project(steps[n + 1])
        weights = [soften(s) for s in scores]
        ones = jnp.ones((BLOCK, head), BF16)
        for e, (r, c) in zip(weights, units):
            both = dot(e, jnp.concatenate([v[r, c], ones], axis=1))
            mix_ref[r, p * pair + c.start : p * pair + c.stop] = (
                both[:, :head] / both[:, head:]
            ).astype(BF16)
        if p + 1 == HEADS // 2:
            finish(t, dot(mix_ref[...], w_out_ref[...]))


def row_kernel(s_ref, gain_ref, bias_ref, w_qkv_ref, w_out_ref, o_ref, h_ref, mix_ref):
    rows, width, channels = s_ref.shape
    dests, _, part, _ = o_ref.shape
    x = s_ref[...].reshape(rows * width, channels).astype(F32)
    inverse = lax.rsqrt(jnp.mean(x * x, axis=-1, keepdims=True) + EPS)
    h_ref[...] = (x * inverse * gain_ref[...] + bias_ref[...]).astype(BF16)

    def finish(_, y):
        y = (y + h_ref[...].astype(F32)).astype(BF16).reshape(rows, width, channels)
        for d in range(dests):
            o_ref[d] = y[:, d * part : (d + 1) * part, :]

    attention(1, rows * width, lambda t: h_ref[...], w_qkv_ref, w_out_ref, mix_ref, finish, None)


def row_call(s, gain, bias, w_qkv, w_out, dests):
    rows, width, channels = s.shape
    step = min(TILE // width, rows)
    part = width // dests
    return pl.pallas_call(
        row_kernel,
        grid=(rows // step,),
        out_shape=jax.ShapeDtypeStruct((dests, rows, part, channels), BF16),
        in_specs=[
            pl.BlockSpec((step, width, channels), lambda i: (i, 0, 0)),
            pl.BlockSpec((1, channels), lambda i: (0, 0)),
            pl.BlockSpec((1, channels), lambda i: (0, 0)),
            pl.BlockSpec(w_qkv.shape, lambda i: (0, 0), pipeline_mode=pl.Buffered(1)),
            pl.BlockSpec(w_out.shape, lambda i: (0, 0), pipeline_mode=pl.Buffered(1)),
        ],
        out_specs=pl.BlockSpec((dests, step, part, channels), lambda i: (0, i, 0, 0)),
        scratch_shapes=[pltpu.VMEM((step * width, channels), BF16)] * 2,
        compiler_params=pltpu.CompilerParams(vmem_limit_bytes=60 << 20),
        cost_estimate=pl.CostEstimate(
            flops=rows * width * channels * (8 * channels + 4 * width),
            bytes_accessed=4 * rows * width * channels + 8 * channels * channels,
            transcendentals=0,
        ),
        name="row_attention",
    )(s, gain, bias, w_qkv, w_out)


def col_kernel(n_chunks, *refs):
    chunks = refs[:n_chunks]
    gain_ref, w_qkv_ref, w_out_ref, o_ref, x_ref, n_ref, mix_ref = refs[n_chunks:]
    rows, cols, channels = o_ref.shape
    sources, deep = chunks[0].shape[:2]
    lanes = channels // 128
    for i, chunk in enumerate(chunks):
        for s in range(sources):
            first = (s * n_chunks + i) * deep
            for c in range(lanes):
                x_ref[c, first * cols : (first + deep) * cols, :] = (
                    chunk[s, :, :, c * 128 : (c + 1) * 128].reshape(deep * cols, 128).astype(F32)
                )
    for w in range(cols):
        x = jnp.concatenate(
            [x_ref[c, pl.ds(w, rows, stride=cols), :] for c in range(lanes)], axis=1
        )
        inverse = lax.rsqrt(jnp.mean(x * x, axis=-1, keepdims=True) + EPS)
        n_ref[w * rows : (w + 1) * rows, :] = (x * inverse * gain_ref[...]).astype(BF16)
    keep = None
    if rows < BLOCK:
        left = lax.broadcasted_iota(jnp.int32, (BLOCK, BLOCK), 0) // rows
        keep = left == lax.broadcasted_iota(jnp.int32, (BLOCK, BLOCK), 1) // rows
    tile = mix_ref.shape[0]
    each = tile // rows

    def finish(t, y):
        for i in range(each):
            for c in range(lanes):
                at = pl.ds(t * each + i, rows, stride=cols)
                x_ref[c, at, :] = (
                    x_ref[c, at, :] + y[i * rows : (i + 1) * rows, c * 128 : (c + 1) * 128]
                )

    attention(
        rows * cols // tile,
        tile,
        lambda t: n_ref[t * tile : (t + 1) * tile, :],
        w_qkv_ref,
        w_out_ref,
        mix_ref,
        finish,
        keep,
    )
    for c in range(lanes):
        o_ref[:, :, c * 128 : (c + 1) * 128] = x_ref[c].astype(BF16).reshape(rows, cols, 128)


def col_call(chunks, gain, w_qkv, w_out):
    sources, deep, cols, channels = chunks[0].shape
    n_chunks = len(chunks)
    rows = sources * deep * n_chunks
    step = min(16, cols)
    tile = min(TILE, rows * step)
    return pl.pallas_call(
        lambda *refs: col_kernel(n_chunks, *refs),
        grid=(cols // step,),
        out_shape=jax.ShapeDtypeStruct((rows, cols, channels), BF16),
        in_specs=[pl.BlockSpec((sources, deep, step, channels), lambda i: (0, 0, i, 0))] * n_chunks
        + [
            pl.BlockSpec((1, channels), lambda i: (0, 0)),
            pl.BlockSpec(w_qkv.shape, lambda i: (0, 0), pipeline_mode=pl.Buffered(1)),
            pl.BlockSpec(w_out.shape, lambda i: (0, 0), pipeline_mode=pl.Buffered(1)),
        ],
        out_specs=pl.BlockSpec((rows, step, channels), lambda i: (0, i, 0)),
        scratch_shapes=[
            pltpu.VMEM((channels // 128, rows * step, 128), F32),
            pltpu.VMEM((rows * step, channels), BF16),
            pltpu.VMEM((tile, channels), BF16),
        ],
        compiler_params=pltpu.CompilerParams(vmem_limit_bytes=60 << 20),
        cost_estimate=pl.CostEstimate(
            flops=rows * cols * channels * (8 * channels + 4 * rows),
            bytes_accessed=4 * rows * cols * channels + 8 * channels * channels,
            transcendentals=0,
        ),
        name="col_attention",
    )(*chunks, gain, w_qkv, w_out)


def on_device(
    latents,
    owners,
    lead_ids,
    film_scale,
    film_shift,
    w_qkv_row,
    w_out_row,
    gain_col,
    w_qkv_col,
    w_out_col,
):
    slab = latents[0]
    dests = lax.axis_size("space")
    own_index = lax.axis_index("lead")
    own_count = jnp.sum((owners == own_index).astype(BF16))
    summed = lax.psum(slab * own_count, "lead")
    film_gain = 1.0 + lax.dynamic_slice_in_dim(film_scale, lead_ids[0], 1, 0)
    film_bias = lax.dynamic_slice_in_dim(film_shift, lead_ids[0], 1, 0)

    def whole(piece):
        return lax.all_gather(piece, "space", axis=0, tiled=True)

    after_rows = row_call(summed, film_gain, film_bias, whole(w_qkv_row), whole(w_out_row), dests)
    columns = lax.all_to_all(after_rows, "space", split_axis=0, concat_axis=0, tiled=True)
    result = col_call([columns], gain_col[None, :], whole(w_qkv_col), whole(w_out_col))
    return result[None]


def solution(mesh):
    placed = (
        P("lead", "space", None, None),
        P(),
        P("lead"),
        P(),
        P(),
        P("space", None),
        P("space", None),
        P(),
        P("space", None),
        P("space", None),
    )
    return jax.shard_map(
        on_device,
        mesh=mesh,
        in_specs=placed,
        out_specs=P("lead", None, "space", None),
        check_vma=False,
    )
```

```python
import math

import jax
import jax.numpy as jnp
from jax import lax
from jax.experimental import pallas as pl
from jax.experimental.pallas import tpu as pltpu
from jax.sharding import PartitionSpec as P


HEADS = 8
EPS = 1e-06
NEG = -1e30
BLOCK = 128
TILE = 512
CHUNKS = 4
F32 = jnp.float32
BF16 = jnp.bfloat16


def dot(a, b):
    return jnp.dot(a, b, preferred_element_type=F32)


def dot_t(a, b):
    return lax.dot_general(a, b, (((1,), (1,)), ((), ())), preferred_element_type=F32)


def fetch(pieces, space, w_ref, sems):
    channels = w_ref.shape[0]
    pair = 2 * channels // HEADS
    groups = [[], [], []]
    for j, (w_qkv, w_out) in enumerate(pieces):
        deep = w_out.shape[0]
        at = pl.ds(pl.multiple_of((space ^ j) * deep, deep), deep)
        for c in range(3):
            for g, low, high in ((0, 0, pair), (1, pair, channels)):
                lane = slice(c * channels + low, c * channels + high)
                groups[g].append(
                    pltpu.make_async_copy(
                        w_qkv.at[:, lane], w_ref.at[at, lane], sems.at[2 * c + g, j]
                    )
                )
        groups[2].append(
            pltpu.make_async_copy(w_out, w_ref.at[at, 3 * channels :], sems.at[6, j])
        )
    return groups


def paired(refs):
    return list(zip(refs[::2], refs[1::2]))


def weight_scratch(channels, n_space):
    return [
        pltpu.VMEM((channels, 4 * channels), BF16),
        pltpu.SemaphoreType.DMA((7, n_space)),
    ]


class Pairs:
    def __init__(self, tokens, channels, keep):
        self.head = channels // HEADS
        self.pair = 2 * self.head
        self.factor = math.log2(math.e) / math.sqrt(self.head)
        self.keep = keep
        self.units = [
            (slice(b * BLOCK, (b + 1) * BLOCK), j * self.head)
            for b in range(tokens // BLOCK)
            for j in range(2)
        ]

    def scores(self, qkv):
        q, k, _ = qkv
        return [
            dot_t(q[r, c : c + self.head], k[r, c : c + self.head]) for r, c in self.units
        ]

    def mix(self, scores, qkv, mix_ref, lane):
        v = qkv[2]
        ones = jnp.ones((BLOCK, self.head), BF16)
        weights = []
        for s in scores:
            if self.keep is not None:
                s = jnp.where(self.keep, s, NEG)
            top = jnp.max(s, axis=-1, keepdims=True)
            weights.append(jnp.exp2((s - top) * self.factor).astype(BF16))
        for e, (r, c) in zip(weights, self.units):
            both = dot(e, jnp.concatenate([v[r, c : c + self.head], ones], axis=1))
            mix_ref[r, lane + c : lane + c + self.head] = (
                both[:, : self.head] / both[:, self.head :]
            ).astype(BF16)

    def project(self, x, w_ref, p):
        channels = w_ref.shape[0]
        first = p * self.pair
        return [
            dot(x, w_ref[:, c * channels + first : c * channels + first + self.pair]).astype(BF16)
            for c in range(3)
        ]


def row_kernel(n_space, place_ref, *refs):
    mine_ref, other_ref, gain_ref, bias_ref = refs[:4]
    pieces = paired(refs[4 : 4 + 2 * n_space])
    outs = refs[4 + 2 * n_space : 4 + 3 * n_space]
    h_ref, mix_ref, y_ref, w_ref, sems = refs[4 + 3 * n_space :]
    half, width, channels = mine_ref.shape
    part = width // n_space
    space = place_ref[0]
    side = place_ref[1]
    groups = fetch(pieces, space, w_ref, sems)
    for group in groups:
        for copy in group:
            copy.start()
    tokens = half * width
    for n, ref in enumerate((mine_ref, other_ref)):
        x = ref[...].reshape(tokens, channels).astype(F32)
        inverse = lax.rsqrt(jnp.mean(x * x, axis=-1, keepdims=True) + EPS)
        h_ref[n * tokens : (n + 1) * tokens, :] = (
            x * inverse * gain_ref[...] + bias_ref[...]
        ).astype(BF16)
    pairs = Pairs(2 * tokens, channels, None)
    for copy in groups[0]:
        copy.wait()
    ahead = pairs.project(h_ref[...], w_ref, 0)
    for p in range(HEADS // 2):
        qkv = ahead
        scores = pairs.scores(qkv)
        if p < 2:
            for copy in groups[p + 1]:
                copy.wait()
        if p + 1 < HEADS // 2:
            ahead = pairs.project(h_ref[...], w_ref, p + 1)
        pairs.mix(scores, qkv, mix_ref, p * pairs.pair)
    y = dot(mix_ref[...], w_ref[:, 3 * channels :])
    y = (y + h_ref[...].astype(F32)).astype(BF16)
    for n in range(2):
        at = pl.ds((side ^ n) * half, half)
        y_ref[at] = y[n * tokens : (n + 1) * tokens].reshape(half, width, channels)
    for j, out in enumerate(outs):
        at = pl.ds(pl.multiple_of((space ^ j) * part, part), part)
        out[...] = y_ref[:, at, :]


def row_call(place, mine, other, gain, bias, pieces):
    half, width, channels = mine.shape
    n_space = len(pieces)
    part = width // n_space
    tokens = 2 * half * width
    vmem = pl.BlockSpec(memory_space=pltpu.VMEM)
    return pl.pallas_call(
        lambda *refs: row_kernel(n_space, *refs),
        out_shape=[jax.ShapeDtypeStruct((2 * half, part, channels), BF16)] * n_space,
        in_specs=[pl.BlockSpec(memory_space=pltpu.SMEM)]
        + [vmem] * 4
        + [pl.BlockSpec(memory_space=pl.ANY)] * (2 * n_space),
        out_specs=[vmem] * n_space,
        scratch_shapes=[
            pltpu.VMEM((tokens, channels), BF16),
            pltpu.VMEM((tokens, channels), BF16),
            pltpu.VMEM((2 * half, width, channels), BF16),
            *weight_scratch(channels, n_space),
        ],
        compiler_params=pltpu.CompilerParams(vmem_limit_bytes=60 << 20),
        cost_estimate=pl.CostEstimate(
            flops=tokens * channels * (8 * channels + 4 * width),
            bytes_accessed=4 * tokens * channels + 8 * channels * channels,
            transcendentals=0,
        ),
        name="row_attention",
    )(place, mine, other, gain, bias, *[w for piece in pieces for w in piece])


def col_kernel(n_chunks, n_space, place_ref, *refs):
    count = n_chunks * n_space
    chunks = refs[:count]
    gain_ref = refs[count]
    pieces = paired(refs[count + 1 : count + 1 + 2 * n_space])
    o_ref, x_ref, n_ref, mix_ref, perm_ref, w_ref, sems = refs[count + 1 + 2 * n_space :]
    rows, cols, channels = o_ref.shape
    deep = chunks[0].shape[0]
    space = place_ref[0]
    groups = fetch(pieces, space, w_ref, sems)
    for group in groups:
        for copy in group:
            copy.start()
    for i in range(n_chunks):
        for j in range(n_space):
            first = ((space ^ j) * n_chunks + i) * deep
            x_ref[pl.ds(first, deep)] = chunks[i * n_space + j][...].astype(F32)
    keep = None
    if rows < BLOCK:
        left = lax.broadcasted_iota(jnp.int32, (BLOCK, BLOCK), 0) // rows
        keep = left == lax.broadcasted_iota(jnp.int32, (BLOCK, BLOCK), 1) // rows
    tokens = mix_ref.shape[0]
    each = tokens // rows
    tiles = cols // each
    pairs = Pairs(tokens, channels, keep)

    here = lax.broadcasted_iota(jnp.int32, (tokens, tokens), 0)
    there = lax.broadcasted_iota(jnp.int32, (tokens, tokens), 1)
    perm_ref[0] = ((here % rows) * each + here // rows == there).astype(BF16)
    perm_ref[1] = ((there % rows) * each + there // rows == here).astype(BF16)

    def wide(t):
        return x_ref[:, t * each : (t + 1) * each, :].reshape(tokens, channels)

    def prepare(t):
        x = wide(t)
        inverse = lax.rsqrt(jnp.mean(x * x, axis=-1, keepdims=True) + EPS)
        normed = (x * inverse * gain_ref[...]).astype(BF16)
        n_ref[t % 2] = dot(perm_ref[0], normed).astype(BF16)

    def finish(t):
        mixed = dot(perm_ref[1], mix_ref[...]).astype(BF16)
        y = wide(t) + dot(mixed, w_ref[:, 3 * channels :])
        x_ref[:, t * each : (t + 1) * each, :] = y.reshape(rows, each, channels)
        if (t + 1) * each % 16 == 0 or t + 1 == tiles:
            at = slice((t + 1) * each - min(16, (t + 1) * each), (t + 1) * each)
            o_ref[:, at, :] = x_ref[:, at, :].astype(BF16)

    prepare(0)
    for copy in groups[0]:
        copy.wait()
    ahead = pairs.project(n_ref[0], w_ref, 0)
    for group in groups[1:]:
        for copy in group:
            copy.wait()
    steps = [(t, p) for t in range(tiles) for p in range(HEADS // 2)]
    for n, (t, p) in enumerate(steps):
        qkv = ahead
        scores = pairs.scores(qkv)
        if n + 1 < len(steps):
            after = steps[n + 1]
            ahead = pairs.project(n_ref[after[0] % 2], w_ref, after[1])
        if p == 1 and t + 1 < tiles:
            prepare(t + 1)
        pairs.mix(scores, qkv, mix_ref, p * pairs.pair)
        if p + 1 == HEADS // 2:
            finish(t)


def col_call(place, chunks, gain, pieces):
    deep, cols, channels = chunks[0][0].shape
    n_chunks = len(chunks)
    n_space = len(pieces)
    rows = n_space * deep * n_chunks
    tokens = min(TILE, rows * cols)
    vmem = pl.BlockSpec(memory_space=pltpu.VMEM)
    return pl.pallas_call(
        lambda *refs: col_kernel(n_chunks, n_space, *refs),
        out_shape=jax.ShapeDtypeStruct((rows, cols, channels), BF16),
        in_specs=[pl.BlockSpec(memory_space=pltpu.SMEM)]
        + [vmem] * (n_chunks * n_space + 1)
        + [pl.BlockSpec(memory_space=pl.ANY)] * (2 * n_space),
        out_specs=vmem,
        scratch_shapes=[
            pltpu.VMEM((rows, cols, channels), F32),
            pltpu.VMEM((2, tokens, channels), BF16),
            pltpu.VMEM((tokens, channels), BF16),
            pltpu.VMEM((2, tokens, tokens), BF16),
            *weight_scratch(channels, n_space),
        ],
        compiler_params=pltpu.CompilerParams(vmem_limit_bytes=60 << 20),
        cost_estimate=pl.CostEstimate(
            flops=rows * cols * channels * (8 * channels + 4 * rows),
            bytes_accessed=4 * rows * cols * channels + 8 * channels * channels,
            transcendentals=0,
        ),
        name="col_attention",
    )(
        place,
        *[piece for chunk in chunks for piece in chunk],
        gain,
        *[w for piece in pieces for w in piece],
    )


def on_device(
    latents,
    owners,
    lead_ids,
    film_scale,
    film_shift,
    w_qkv_row,
    w_out_row,
    gain_col,
    w_qkv_col,
    w_out_col,
):
    slab = latents[0]
    rows, _, _ = slab.shape
    n_lead = lax.axis_size("lead")
    n_space = lax.axis_size("space")
    lead = lax.axis_index("lead")
    space = lax.axis_index("space")
    side = lead % 2
    depth = n_lead // 2
    chunks = chunk_count(rows)
    half = rows // (2 * chunks)
    place = jnp.stack([space, side]).astype(jnp.int32)
    owned = jnp.sum((owners == lead).astype(BF16))

    def own_half(i, which):
        return lax.dynamic_slice_in_dim(slab, (2 * i + which) * half, half, 0) * owned

    sends, keeps = lax.optimization_barrier(
        ([own_half(i, 1 - side) for i in range(chunks)], [own_half(i, side) for i in range(chunks)])
    )
    swap = [(l, l ^ 1) for l in range(n_lead)]
    hops = [
        [
            pair
            for s in range(2)
            for pair in (
                ((depth - h) * 2 + s, (depth - h - 1) * 2 + s),
                ((h - 1) * 2 + s, h * 2 + s),
            )
        ]
        for h in range(1, depth)
    ]

    def across(value, j):
        return lax.ppermute(value, "space", [(s, s ^ j) for s in range(n_space)])

    bits = [1 << b for b in reversed(range(n_space.bit_length() - 1))]

    def spread(held, bit):
        return {**held, **{j ^ bit: [across(w, bit) for w in v] for j, v in held.items()}}

    film_gain = 1.0 + lax.dynamic_slice_in_dim(film_scale, lead_ids[0], 1, 0)
    film_bias = lax.dynamic_slice_in_dim(film_shift, lead_ids[0], 1, 0)
    row_held = {0: [w_qkv_row, w_out_row]}
    col_held = {0: [w_qkv_col, w_out_col]}

    row_held = spread(row_held, bits[0])
    col_held = spread(col_held, bits[0])
    for bit in bits[1:]:
        row_held = spread(row_held, bit)
        col_held = spread(col_held, bit)
    row_pieces = [row_held[j] for j in range(n_space)]

    exchanged = []
    for i in range(chunks):
        got = lax.ppermute(sends[i], "lead", swap)
        own = keeps[i] + got
        terms = [own]
        for h, pairs in enumerate(hops):
            send = own if h == 0 else own + terms[-1]
            terms.append(lax.ppermute(send, "lead", pairs))
        mine = terms[0]
        for got in terms[1:]:
            mine = mine + got
        other = lax.ppermute(mine, "lead", swap)
        outs = row_call(place, mine, other, film_gain, film_bias, row_pieces)
        exchanged.append([outs[0]] + [across(outs[j], j) for j in range(1, n_space)])

    result = col_call(
        place,
        exchanged,
        gain_col[None, :],
        [col_held[j] for j in range(n_space)],
    )
    return result[None]


def chunk_count(rows):
    return min(CHUNKS, rows // 2)


def solution(mesh):
    placed = (
        P("lead", "space", None, None),
        P(),
        P("lead"),
        P(),
        P(),
        P("space", None),
        P("space", None),
        P(),
        P("space", None),
        P("space", None),
    )

    return jax.shard_map(
        on_device,
        mesh=mesh,
        in_specs=placed,
        out_specs=P("lead", None, "space", None),
        check_vma=False,
    )
```

```python
import math

import jax
import jax.numpy as jnp
from jax import lax
from jax.experimental import pallas as pl
from jax.experimental.pallas import tpu as pltpu
from jax.sharding import PartitionSpec as P


HEADS = 8
EPS = 1e-06
NEG = -1e30
BLOCK = 128
TILE = 512
CHUNKS = 4
F32 = jnp.float32
BF16 = jnp.bfloat16


def dot(a, b):
    return jnp.dot(a, b, preferred_element_type=F32)


def dot_t(a, b):
    return lax.dot_general(a, b, (((1,), (1,)), ((), ())), preferred_element_type=F32)


def fetch(pieces, space, w_ref, sems):
    channels = w_ref.shape[0]
    pair = 2 * channels // HEADS
    groups = [[], [], []]
    for j, (w_qkv, w_out) in enumerate(pieces):
        deep = w_out.shape[0]
        at = pl.ds(pl.multiple_of((space ^ j) * deep, deep), deep)
        for c in range(3):
            for g, low, high in ((0, 0, pair), (1, pair, channels)):
                lane = slice(c * channels + low, c * channels + high)
                groups[g].append(
                    pltpu.make_async_copy(
                        w_qkv.at[:, lane], w_ref.at[at, lane], sems.at[2 * c + g, j]
                    )
                )
        groups[2].append(
            pltpu.make_async_copy(w_out, w_ref.at[at, 3 * channels :], sems.at[6, j])
        )
    return groups


def paired(refs):
    return list(zip(refs[::2], refs[1::2]))


def weight_scratch(channels, n_space):
    return [
        pltpu.VMEM((channels, 4 * channels), BF16),
        pltpu.SemaphoreType.DMA((7, n_space)),
    ]


class Pairs:
    def __init__(self, tokens, channels, keep):
        self.head = channels // HEADS
        self.pair = 2 * self.head
        self.factor = math.log2(math.e) / math.sqrt(self.head)
        self.keep = keep
        self.units = [
            (slice(b * BLOCK, (b + 1) * BLOCK), j * self.head)
            for b in range(tokens // BLOCK)
            for j in range(2)
        ]

    def scores(self, qkv):
        q, k, _ = qkv
        return [
            dot_t(q[r, c : c + self.head], k[r, c : c + self.head]) for r, c in self.units
        ]

    def mix(self, scores, qkv, mix_ref, lane):
        v = qkv[2]
        ones = jnp.ones((BLOCK, self.head), BF16)
        weights = []
        for s in scores:
            if self.keep is not None:
                s = jnp.where(self.keep, s, NEG)
            top = jnp.max(s, axis=-1, keepdims=True)
            weights.append(jnp.exp2((s - top) * self.factor).astype(BF16))
        for e, (r, c) in zip(weights, self.units):
            both = dot(e, jnp.concatenate([v[r, c : c + self.head], ones], axis=1))
            mix_ref[r, pl.ds(lane + c, self.head)] = (
                both[:, : self.head] / both[:, self.head :]
            ).astype(BF16)

    def project(self, x, w_ref, p):
        channels = w_ref.shape[0]
        first = p * self.pair
        if not isinstance(p, int):
            first = pl.multiple_of(first, self.pair)
        return [
            dot(x, w_ref[:, pl.ds(c * channels + first, self.pair)]).astype(BF16)
            for c in range(3)
        ]


def row_kernel(n_space, place_ref, *refs):
    mine_ref, other_ref, gain_ref, bias_ref = refs[:4]
    pieces = paired(refs[4 : 4 + 2 * n_space])
    outs = refs[4 + 2 * n_space : 4 + 3 * n_space]
    h_ref, mix_ref, y_ref, qkv_ref, w_ref, sems = refs[4 + 3 * n_space :]
    half, width, channels = mine_ref.shape
    part = width // n_space
    space = place_ref[0]
    side = place_ref[1]
    groups = fetch(pieces, space, w_ref, sems)
    for group in groups:
        for copy in group:
            copy.start()
    tokens = half * width
    for n, ref in enumerate((mine_ref, other_ref)):
        x = ref[...].reshape(tokens, channels).astype(F32)
        inverse = lax.rsqrt(jnp.mean(x * x, axis=-1, keepdims=True) + EPS)
        h_ref[n * tokens : (n + 1) * tokens, :] = (
            x * inverse * gain_ref[...] + bias_ref[...]
        ).astype(BF16)
    pairs = Pairs(2 * tokens, channels, None)
    for copy in groups[0]:
        copy.wait()
    last = HEADS // 2 - 1
    for c, value in enumerate(pairs.project(h_ref[...], w_ref, 0)):
        qkv_ref[c] = value
    for copy in groups[1]:
        copy.wait()

    def body(p, _):
        qkv = [qkv_ref[c] for c in range(3)]
        scores = pairs.scores(qkv)
        ahead = pairs.project(h_ref[...], w_ref, p + 1)
        pairs.mix(scores, qkv, mix_ref, pl.multiple_of(p * pairs.pair, pairs.pair))
        for c, value in enumerate(ahead):
            qkv_ref[c] = value

    lax.fori_loop(0, last, body, None)
    for copy in groups[2]:
        copy.wait()
    qkv = [qkv_ref[c] for c in range(3)]
    pairs.mix(pairs.scores(qkv), qkv, mix_ref, last * pairs.pair)
    y = dot(mix_ref[...], w_ref[:, 3 * channels :])
    y = (y + h_ref[...].astype(F32)).astype(BF16)
    for n in range(2):
        at = pl.ds((side ^ n) * half, half)
        y_ref[at] = y[n * tokens : (n + 1) * tokens].reshape(half, width, channels)
    for j, out in enumerate(outs):
        at = pl.ds(pl.multiple_of((space ^ j) * part, part), part)
        out[...] = y_ref[:, at, :]


def row_call(place, mine, other, gain, bias, pieces):
    half, width, channels = mine.shape
    n_space = len(pieces)
    part = width // n_space
    tokens = 2 * half * width
    vmem = pl.BlockSpec(memory_space=pltpu.VMEM)
    return pl.pallas_call(
        lambda *refs: row_kernel(n_space, *refs),
        out_shape=[jax.ShapeDtypeStruct((2 * half, part, channels), BF16)] * n_space,
        in_specs=[pl.BlockSpec(memory_space=pltpu.SMEM)]
        + [vmem] * 4
        + [pl.BlockSpec(memory_space=pl.ANY)] * (2 * n_space),
        out_specs=[vmem] * n_space,
        scratch_shapes=[
            pltpu.VMEM((tokens, channels), BF16),
            pltpu.VMEM((tokens, channels), BF16),
            pltpu.VMEM((2 * half, width, channels), BF16),
            pltpu.VMEM((3, tokens, 2 * channels // HEADS), BF16),
            *weight_scratch(channels, n_space),
        ],
        compiler_params=pltpu.CompilerParams(vmem_limit_bytes=60 << 20),
        cost_estimate=pl.CostEstimate(
            flops=tokens * channels * (8 * channels + 4 * width),
            bytes_accessed=4 * tokens * channels + 8 * channels * channels,
            transcendentals=0,
        ),
        name="row_attention",
    )(place, mine, other, gain, bias, *[w for piece in pieces for w in piece])


def col_kernel(n_chunks, n_space, place_ref, *refs):
    count = n_chunks * n_space
    chunks = refs[:count]
    gain_ref = refs[count]
    pieces = paired(refs[count + 1 : count + 1 + 2 * n_space])
    o_ref, x_ref, n_ref, mix_ref, perm_ref, qkv_ref, w_ref, sems = refs[count + 1 + 2 * n_space :]
    rows, cols, channels = o_ref.shape
    deep = chunks[0].shape[0]
    space = place_ref[0]
    groups = fetch(pieces, space, w_ref, sems)
    for group in groups:
        for copy in group:
            copy.start()
    for i in range(n_chunks):
        for j in range(n_space):
            first = ((space ^ j) * n_chunks + i) * deep
            x_ref[pl.ds(first, deep)] = chunks[i * n_space + j][...].astype(F32)
    keep = None
    if rows < BLOCK:
        left = lax.broadcasted_iota(jnp.int32, (BLOCK, BLOCK), 0) // rows
        keep = left == lax.broadcasted_iota(jnp.int32, (BLOCK, BLOCK), 1) // rows
    tokens = mix_ref.shape[0]
    each = tokens // rows
    tiles = cols // each
    pairs = Pairs(tokens, channels, keep)

    here = lax.broadcasted_iota(jnp.int32, (tokens, tokens), 0)
    there = lax.broadcasted_iota(jnp.int32, (tokens, tokens), 1)
    perm_ref[0] = ((here % rows) * each + here // rows == there).astype(BF16)
    perm_ref[1] = ((there % rows) * each + there // rows == here).astype(BF16)

    def place_of(t):
        return pl.ds(pl.multiple_of(t * each, each), each)

    def wide(t):
        return x_ref[:, place_of(t), :].reshape(tokens, channels)

    def prepare(t):
        x = wide(t)
        inverse = lax.rsqrt(jnp.mean(x * x, axis=-1, keepdims=True) + EPS)
        normed = (x * inverse * gain_ref[...]).astype(BF16)
        n_ref[...] = dot(perm_ref[0], normed).astype(BF16)

    def keep_ahead(values):
        for c, value in enumerate(values):
            qkv_ref[c] = value

    last = HEADS // 2 - 1

    def tile(t, _):
        ahead = [qkv_ref[c] for c in range(3)]
        for p in range(last + 1):
            qkv = ahead
            scores = pairs.scores(qkv)
            if p < last:
                ahead = pairs.project(n_ref[...], w_ref, p + 1)
            else:
                keep_ahead(pairs.project(n_ref[...], w_ref, 0))
            if p == last - 1:
                prepare(jnp.minimum(t + 1, tiles - 1))
            pairs.mix(scores, qkv, mix_ref, p * pairs.pair)
        mixed = dot(perm_ref[1], mix_ref[...]).astype(BF16)
        y = wide(t) + dot(mixed, w_ref[:, 3 * channels :])
        x_ref[:, place_of(t), :] = y.reshape(rows, each, channels)

    prepare(0)
    for copy in groups[0]:
        copy.wait()
    keep_ahead(pairs.project(n_ref[...], w_ref, 0))
    for group in groups[1:]:
        for copy in group:
            copy.wait()
    lax.fori_loop(0, tiles, tile, None)
    o_ref[...] = x_ref[...].astype(BF16)


def col_call(place, chunks, gain, pieces):
    deep, cols, channels = chunks[0][0].shape
    n_chunks = len(chunks)
    n_space = len(pieces)
    rows = n_space * deep * n_chunks
    tokens = min(TILE, rows * cols)
    vmem = pl.BlockSpec(memory_space=pltpu.VMEM)
    return pl.pallas_call(
        lambda *refs: col_kernel(n_chunks, n_space, *refs),
        out_shape=jax.ShapeDtypeStruct((rows, cols, channels), BF16),
        in_specs=[pl.BlockSpec(memory_space=pltpu.SMEM)]
        + [vmem] * (n_chunks * n_space + 1)
        + [pl.BlockSpec(memory_space=pl.ANY)] * (2 * n_space),
        out_specs=vmem,
        scratch_shapes=[
            pltpu.VMEM((rows, cols, channels), F32),
            pltpu.VMEM((tokens, channels), BF16),
            pltpu.VMEM((tokens, channels), BF16),
            pltpu.VMEM((2, tokens, tokens), BF16),
            pltpu.VMEM((3, tokens, 2 * channels // HEADS), BF16),
            *weight_scratch(channels, n_space),
        ],
        compiler_params=pltpu.CompilerParams(vmem_limit_bytes=60 << 20),
        cost_estimate=pl.CostEstimate(
            flops=rows * cols * channels * (8 * channels + 4 * rows),
            bytes_accessed=4 * rows * cols * channels + 8 * channels * channels,
            transcendentals=0,
        ),
        name="col_attention",
    )(
        place,
        *[piece for chunk in chunks for piece in chunk],
        gain,
        *[w for piece in pieces for w in piece],
    )


def on_device(
    latents,
    owners,
    lead_ids,
    film_scale,
    film_shift,
    w_qkv_row,
    w_out_row,
    gain_col,
    w_qkv_col,
    w_out_col,
):
    slab = latents[0]
    rows, _, _ = slab.shape
    n_lead = lax.axis_size("lead")
    n_space = lax.axis_size("space")
    lead = lax.axis_index("lead")
    space = lax.axis_index("space")
    side = lead % 2
    depth = n_lead // 2
    chunks = chunk_count(rows)
    half = rows // (2 * chunks)
    place = jnp.stack([space, side]).astype(jnp.int32)
    owned = jnp.sum((owners == lead).astype(BF16))

    def own_half(i, which):
        return lax.dynamic_slice_in_dim(slab, (2 * i + which) * half, half, 0) * owned

    sends, keeps = lax.optimization_barrier(
        ([own_half(i, 1 - side) for i in range(chunks)], [own_half(i, side) for i in range(chunks)])
    )
    swap = [(l, l ^ 1) for l in range(n_lead)]
    hops = [
        [
            pair
            for s in range(2)
            for pair in (
                ((depth - h) * 2 + s, (depth - h - 1) * 2 + s),
                ((h - 1) * 2 + s, h * 2 + s),
            )
        ]
        for h in range(1, depth)
    ]

    def across(value, j):
        return lax.ppermute(value, "space", [(s, s ^ j) for s in range(n_space)])

    bits = [1 << b for b in reversed(range(n_space.bit_length() - 1))]

    def spread(held, bit):
        return {**held, **{j ^ bit: [across(w, bit) for w in v] for j, v in held.items()}}

    film_gain = 1.0 + lax.dynamic_slice_in_dim(film_scale, lead_ids[0], 1, 0)
    film_bias = lax.dynamic_slice_in_dim(film_shift, lead_ids[0], 1, 0)
    row_held = {0: [w_qkv_row, w_out_row]}
    col_held = {0: [w_qkv_col, w_out_col]}

    row_held = spread(row_held, bits[0])
    col_held = spread(col_held, bits[0])
    for bit in bits[1:]:
        row_held = spread(row_held, bit)
        col_held = spread(col_held, bit)
    row_pieces = [row_held[j] for j in range(n_space)]

    exchanged = []
    for i in range(chunks):
        got = lax.ppermute(sends[i], "lead", swap)
        own = keeps[i] + got
        terms = [own]
        for h, pairs in enumerate(hops):
            send = own if h == 0 else own + terms[-1]
            terms.append(lax.ppermute(send, "lead", pairs))
        mine = terms[0]
        for got in terms[1:]:
            mine = mine + got
        other = lax.ppermute(mine, "lead", swap)
        outs = row_call(place, mine, other, film_gain, film_bias, row_pieces)
        exchanged.append([outs[0]] + [across(outs[j], j) for j in range(1, n_space)])

    result = col_call(
        place,
        exchanged,
        gain_col[None, :],
        [col_held[j] for j in range(n_space)],
    )
    return result[None]


def chunk_count(rows):
    return min(CHUNKS, rows // 2)


def solution(mesh):
    placed = (
        P("lead", "space", None, None),
        P(),
        P("lead"),
        P(),
        P(),
        P("space", None),
        P("space", None),
        P(),
        P("space", None),
        P("space", None),
    )

    return jax.shard_map(
        on_device,
        mesh=mesh,
        in_specs=placed,
        out_specs=P("lead", None, "space", None),
        check_vma=False,
    )
```

```python
import math

import jax
import jax.numpy as jnp
from jax import lax
from jax.experimental import pallas as pl
from jax.experimental.pallas import tpu as pltpu
from jax.sharding import PartitionSpec as P


HEADS = 8
EPS = 1e-06
NEG = -1e30
BLOCK = 128
TILE = 512
CHUNKS = 4
F32 = jnp.float32
BF16 = jnp.bfloat16


def dot(a, b):
    return jnp.dot(a, b, preferred_element_type=F32)


def dot_t(a, b):
    return lax.dot_general(a, b, (((1,), (1,)), ((), ())), preferred_element_type=F32)


def fetch(pieces, space, w_ref, sems):
    channels = w_ref.shape[0]
    pair = 2 * channels // HEADS
    groups = [[], [], []]
    for j, (w_qkv, w_out) in enumerate(pieces):
        deep = w_out.shape[0]
        at = pl.ds(pl.multiple_of((space ^ j) * deep, deep), deep)
        for c in range(3):
            for g, low, high in ((0, 0, pair), (1, pair, channels)):
                lane = slice(c * channels + low, c * channels + high)
                groups[g].append(
                    pltpu.make_async_copy(
                        w_qkv.at[:, lane], w_ref.at[at, lane], sems.at[2 * c + g, j]
                    )
                )
        groups[2].append(
            pltpu.make_async_copy(w_out, w_ref.at[at, 3 * channels :], sems.at[6, j])
        )
    return groups


def paired(refs):
    return list(zip(refs[::2], refs[1::2]))


def weight_scratch(channels, n_space):
    return [
        pltpu.VMEM((channels, 4 * channels), BF16),
        pltpu.SemaphoreType.DMA((7, n_space)),
    ]


class Pairs:
    def __init__(self, tokens, channels, keep):
        self.head = channels // HEADS
        self.pair = 2 * self.head
        self.factor = math.log2(math.e) / math.sqrt(self.head)
        self.keep = keep
        self.units = [
            (slice(b * BLOCK, (b + 1) * BLOCK), j * self.head)
            for b in range(tokens // BLOCK)
            for j in range(2)
        ]

    def scores(self, qkv):
        q, k, _ = qkv
        return [
            dot_t(q[r, c : c + self.head], k[r, c : c + self.head]) for r, c in self.units
        ]

    def mix(self, scores, qkv, mix_ref, lane):
        v = qkv[2]
        ones = jnp.ones((BLOCK, self.head), BF16)
        weights = []
        for s in scores:
            if self.keep is not None:
                s = jnp.where(self.keep, s, NEG)
            top = jnp.max(s, axis=-1, keepdims=True)
            weights.append(jnp.exp2((s - top) * self.factor).astype(BF16))
        for e, (r, c) in zip(weights, self.units):
            both = dot(e, jnp.concatenate([v[r, c : c + self.head], ones], axis=1))
            mix_ref[r, pl.ds(lane + c, self.head)] = (
                both[:, : self.head] / both[:, self.head :]
            ).astype(BF16)

    def project(self, x, w_ref, p):
        channels = w_ref.shape[0]
        first = p * self.pair
        if not isinstance(p, int):
            first = pl.multiple_of(first, self.pair)
        return [
            dot(x, w_ref[:, pl.ds(c * channels + first, self.pair)]).astype(BF16)
            for c in range(3)
        ]


def row_kernel(n_space, place_ref, *refs):
    mine_ref, other_ref, gain_ref, bias_ref = refs[:4]
    pieces = paired(refs[4 : 4 + 2 * n_space])
    outs = refs[4 + 2 * n_space : 4 + 3 * n_space]
    h_ref, mix_ref, y_ref, qkv_ref, w_ref, sems = refs[4 + 3 * n_space :]
    half, width, channels = mine_ref.shape
    part = width // n_space
    space = place_ref[0]
    side = place_ref[1]
    groups = fetch(pieces, space, w_ref, sems)
    for group in groups:
        for copy in group:
            copy.start()
    tokens = half * width
    for n, ref in enumerate((mine_ref, other_ref)):
        x = ref[...].reshape(tokens, channels).astype(F32)
        inverse = lax.rsqrt(jnp.mean(x * x, axis=-1, keepdims=True) + EPS)
        h_ref[n * tokens : (n + 1) * tokens, :] = (
            x * inverse * gain_ref[...] + bias_ref[...]
        ).astype(BF16)
    pairs = Pairs(2 * tokens, channels, None)
    for copy in groups[0]:
        copy.wait()
    last = HEADS // 2 - 1
    for c, value in enumerate(pairs.project(h_ref[...], w_ref, 0)):
        qkv_ref[c] = value
    for copy in groups[1]:
        copy.wait()

    def body(p, _):
        qkv = [qkv_ref[c] for c in range(3)]
        scores = pairs.scores(qkv)
        ahead = pairs.project(h_ref[...], w_ref, p + 1)
        pairs.mix(scores, qkv, mix_ref, pl.multiple_of(p * pairs.pair, pairs.pair))
        for c, value in enumerate(ahead):
            qkv_ref[c] = value

    lax.fori_loop(0, last, body, None)
    for copy in groups[2]:
        copy.wait()
    qkv = [qkv_ref[c] for c in range(3)]
    pairs.mix(pairs.scores(qkv), qkv, mix_ref, last * pairs.pair)
    y = dot(mix_ref[...], w_ref[:, 3 * channels :])
    y = (y + h_ref[...].astype(F32)).astype(BF16)
    for n in range(2):
        at = pl.ds((side ^ n) * half, half)
        y_ref[at] = y[n * tokens : (n + 1) * tokens].reshape(half, width, channels)
    for j, out in enumerate(outs):
        at = pl.ds(pl.multiple_of((space ^ j) * part, part), part)
        out[...] = y_ref[:, at, :]


def row_call(place, mine, other, gain, bias, pieces):
    half, width, channels = mine.shape
    n_space = len(pieces)
    part = width // n_space
    tokens = 2 * half * width
    vmem = pl.BlockSpec(memory_space=pltpu.VMEM)
    return pl.pallas_call(
        lambda *refs: row_kernel(n_space, *refs),
        out_shape=[jax.ShapeDtypeStruct((2 * half, part, channels), BF16)] * n_space,
        in_specs=[pl.BlockSpec(memory_space=pltpu.SMEM)]
        + [vmem] * 4
        + [pl.BlockSpec(memory_space=pl.ANY)] * (2 * n_space),
        out_specs=[vmem] * n_space,
        scratch_shapes=[
            pltpu.VMEM((tokens, channels), BF16),
            pltpu.VMEM((tokens, channels), BF16),
            pltpu.VMEM((2 * half, width, channels), BF16),
            pltpu.VMEM((3, tokens, 2 * channels // HEADS), BF16),
            *weight_scratch(channels, n_space),
        ],
        compiler_params=pltpu.CompilerParams(vmem_limit_bytes=28 << 20),
        cost_estimate=pl.CostEstimate(
            flops=tokens * channels * (8 * channels + 4 * width),
            bytes_accessed=4 * tokens * channels + 8 * channels * channels,
            transcendentals=0,
        ),
        name="row_attention",
    )(place, mine, other, gain, bias, *[w for piece in pieces for w in piece])


def col_kernel(n_chunks, n_space, place_ref, *refs):
    count = n_chunks * n_space
    chunks = refs[:count]
    gain_ref = refs[count]
    pieces = paired(refs[count + 1 : count + 1 + 2 * n_space])
    o_ref, x_ref, n_ref, mix_ref, perm_ref, qkv_ref, w_ref, sems = refs[count + 1 + 2 * n_space :]
    rows, cols, channels = o_ref.shape
    deep = chunks[0].shape[0]
    space = place_ref[0]
    groups = fetch(pieces, space, w_ref, sems)
    for group in groups:
        for copy in group:
            copy.start()
    for i in range(n_chunks):
        for j in range(n_space):
            first = ((space ^ j) * n_chunks + i) * deep
            x_ref[pl.ds(first, deep)] = chunks[i * n_space + j][...].astype(F32)
    keep = None
    if rows < BLOCK:
        left = lax.broadcasted_iota(jnp.int32, (BLOCK, BLOCK), 0) // rows
        keep = left == lax.broadcasted_iota(jnp.int32, (BLOCK, BLOCK), 1) // rows
    tokens = mix_ref.shape[0]
    each = tokens // rows
    tiles = cols // each
    pairs = Pairs(tokens, channels, keep)

    here = lax.broadcasted_iota(jnp.int32, (tokens, tokens), 0)
    there = lax.broadcasted_iota(jnp.int32, (tokens, tokens), 1)
    perm_ref[0] = ((here % rows) * each + here // rows == there).astype(BF16)
    perm_ref[1] = ((there % rows) * each + there // rows == here).astype(BF16)

    def place_of(t):
        return pl.ds(pl.multiple_of(t * each, each), each)

    def wide(t):
        return x_ref[:, place_of(t), :].reshape(tokens, channels)

    def prepare(t):
        x = wide(t)
        inverse = lax.rsqrt(jnp.mean(x * x, axis=-1, keepdims=True) + EPS)
        normed = (x * inverse * gain_ref[...]).astype(BF16)
        n_ref[...] = dot(perm_ref[0], normed).astype(BF16)

    def keep_ahead(values):
        for c, value in enumerate(values):
            qkv_ref[c] = value

    last = HEADS // 2 - 1

    def tile(t, _):
        ahead = [qkv_ref[c] for c in range(3)]
        for p in range(last + 1):
            qkv = ahead
            scores = pairs.scores(qkv)
            if p < last:
                ahead = pairs.project(n_ref[...], w_ref, p + 1)
            else:
                keep_ahead(pairs.project(n_ref[...], w_ref, 0))
            if p == last - 1:
                prepare(jnp.minimum(t + 1, tiles - 1))
            pairs.mix(scores, qkv, mix_ref, p * pairs.pair)
        mixed = dot(perm_ref[1], mix_ref[...]).astype(BF16)
        y = wide(t) + dot(mixed, w_ref[:, 3 * channels :])
        x_ref[:, place_of(t), :] = y.reshape(rows, each, channels)

    prepare(0)
    for copy in groups[0]:
        copy.wait()
    keep_ahead(pairs.project(n_ref[...], w_ref, 0))
    for group in groups[1:]:
        for copy in group:
            copy.wait()
    lax.fori_loop(0, tiles, tile, None)
    o_ref[...] = x_ref[...].astype(BF16)


def col_call(place, chunks, gain, pieces):
    deep, cols, channels = chunks[0][0].shape
    n_chunks = len(chunks)
    n_space = len(pieces)
    rows = n_space * deep * n_chunks
    tokens = min(TILE, rows * cols)
    vmem = pl.BlockSpec(memory_space=pltpu.VMEM)
    return pl.pallas_call(
        lambda *refs: col_kernel(n_chunks, n_space, *refs),
        out_shape=jax.ShapeDtypeStruct((rows, cols, channels), BF16),
        in_specs=[pl.BlockSpec(memory_space=pltpu.SMEM)]
        + [vmem] * (n_chunks * n_space + 1)
        + [pl.BlockSpec(memory_space=pl.ANY)] * (2 * n_space),
        out_specs=vmem,
        scratch_shapes=[
            pltpu.VMEM((rows, cols, channels), F32),
            pltpu.VMEM((tokens, channels), BF16),
            pltpu.VMEM((tokens, channels), BF16),
            pltpu.VMEM((2, tokens, tokens), BF16),
            pltpu.VMEM((3, tokens, 2 * channels // HEADS), BF16),
            *weight_scratch(channels, n_space),
        ],
        compiler_params=pltpu.CompilerParams(vmem_limit_bytes=48 << 20),
        cost_estimate=pl.CostEstimate(
            flops=rows * cols * channels * (8 * channels + 4 * rows),
            bytes_accessed=4 * rows * cols * channels + 8 * channels * channels,
            transcendentals=0,
        ),
        name="col_attention",
    )(
        place,
        *[piece for chunk in chunks for piece in chunk],
        gain,
        *[w for piece in pieces for w in piece],
    )


def on_device(
    latents,
    owners,
    lead_ids,
    film_scale,
    film_shift,
    w_qkv_row,
    w_out_row,
    gain_col,
    w_qkv_col,
    w_out_col,
):
    slab = latents[0]
    rows, _, _ = slab.shape
    n_lead = lax.axis_size("lead")
    n_space = lax.axis_size("space")
    lead = lax.axis_index("lead")
    space = lax.axis_index("space")
    side = lead % 2
    depth = n_lead // 2
    chunks = chunk_count(rows)
    half = rows // (2 * chunks)
    place = jnp.stack([space, side]).astype(jnp.int32)
    owned = jnp.sum((owners == lead).astype(BF16))

    def own_half(i, which):
        return lax.dynamic_slice_in_dim(slab, (2 * i + which) * half, half, 0) * owned

    first, owned = lax.optimization_barrier((own_half(0, 1 - side), owned))
    sends, keeps = lax.optimization_barrier(
        ([own_half(i, 1 - side) for i in range(1, chunks)], [own_half(i, side) for i in range(chunks)])
    )
    sends = [first] + sends
    swap = [(l, l ^ 1) for l in range(n_lead)]
    hops = [
        [
            pair
            for s in range(2)
            for pair in (
                ((depth - h) * 2 + s, (depth - h - 1) * 2 + s),
                ((h - 1) * 2 + s, h * 2 + s),
            )
        ]
        for h in range(1, depth)
    ]

    def across(value, j):
        return lax.ppermute(value, "space", [(s, s ^ j) for s in range(n_space)])

    bits = [1 << b for b in reversed(range(n_space.bit_length() - 1))]

    def spread(held, bit):
        return {**held, **{j ^ bit: [across(w, bit) for w in v] for j, v in held.items()}}

    film_gain = 1.0 + lax.dynamic_slice_in_dim(film_scale, lead_ids[0], 1, 0)
    film_bias = lax.dynamic_slice_in_dim(film_shift, lead_ids[0], 1, 0)
    row_held = {0: [w_qkv_row, w_out_row]}
    col_held = {0: [w_qkv_col, w_out_col]}

    row_held = spread(row_held, bits[0])
    col_held = spread(col_held, bits[0])
    for bit in bits[1:]:
        row_held = spread(row_held, bit)
        col_held = spread(col_held, bit)
    row_pieces = [row_held[j] for j in range(n_space)]

    exchanged = []
    for i in range(chunks):
        got = lax.ppermute(sends[i], "lead", swap)
        own = keeps[i] + got
        terms = [own]
        for h, pairs in enumerate(hops):
            send = own if h == 0 else own + terms[-1]
            terms.append(lax.ppermute(send, "lead", pairs))
        mine = terms[0]
        for got in terms[1:]:
            mine = mine + got
        other = lax.ppermute(mine, "lead", swap)
        outs = row_call(place, mine, other, film_gain, film_bias, row_pieces)
        exchanged.append([outs[0]] + [across(outs[j], j) for j in range(1, n_space)])

    result = col_call(
        place,
        exchanged,
        gain_col[None, :],
        [col_held[j] for j in range(n_space)],
    )
    return result[None]


def chunk_count(rows):
    return min(CHUNKS, rows // 2)


def solution(mesh):
    placed = (
        P("lead", "space", None, None),
        P(),
        P("lead"),
        P(),
        P(),
        P("space", None),
        P("space", None),
        P(),
        P("space", None),
        P("space", None),
    )

    return jax.shard_map(
        on_device,
        mesh=mesh,
        in_specs=placed,
        out_specs=P("lead", None, "space", None),
        check_vma=False,
    )
```
